32 devices in a mesh: grp: 2 (over y), wide: 8 (over z, x), tm: 2 (over core).
Axes of the slice: x: 2, y: 2, z: 4, core: 2. Of those that a mesh axis runs over, the one named last changes fastest.
Arguments:
- voltages: bfloat16 [2048, 65536], P('wide', ('grp', 'tm')), parts along dimension 1, may hold values from -6 to 6
- channels: int32 [16], replicated, may hold values from 0 to 1023, as said below
- tile_pairs: int32 [128, 2], replicated, may hold values from 0 to 31, as said below
Outputs:
- visibility: bfloat16 [32, 128, 64, 128], P(('grp', 'wide', 'tm')), parts along dimension 0
The draws below stay inside these ranges and needn't reach their ends.
There are 2 independent parts, one for each index of `grp`. The reference program is written for one: setup_inputs(seed, part) draws one part's arguments, and reference() takes and returns one part's arrays. A program takes and returns all parts, laid end to end along the dimension named above; an argument that names none is the same for every part. Nothing has to cross between parts.
Inputs may be any that keep to these rules, and one draw needn't show every extreme that they name: `channels`: 16 different channel numbers in no fixed order; 0 and 1023 are always among them. `tile_pairs`: 128 different ordered tile pairs; (0, 0) and (31, 31) are always among them.
All inputs are finite; a program needn't handle non-finite values.
Results may differ from the reference program's by a relative error of at most 0.0071.
Values may be sent and summed in bfloat16 or wider, within the bound.
A program may use at most 64 MiB of HBM per device.

```python
import jax
import jax.numpy as jnp
from jax import lax

INPUTS = 2048
TILE = 64
NFFT = 2048
NCHAN = 1024
TILES = 32
NPAIR = 128
FRAMES = 16
SEL = 16


def draw_channels(key, part):
    interior = jax.random.permutation(key, jnp.arange(1, NCHAN - 1, dtype=jnp.int32))[:SEL - 2]
    picked = jnp.concatenate([interior, jnp.array([0, NCHAN - 1], dtype=jnp.int32)])
    return jax.random.permutation(jax.random.fold_in(key, 7), picked)


def draw_tile_pairs(key, part):
    interior = jax.random.permutation(key, jnp.arange(1, TILES * TILES - 1, dtype=jnp.int32))[:NPAIR - 2]
    picked = jnp.concatenate([interior, jnp.array([0, TILES * TILES - 1], dtype=jnp.int32)])
    picked = jax.random.permutation(jax.random.fold_in(key, 11), picked)
    return jnp.stack([picked // TILES, picked % TILES], 1)


def block_levels(own_key, dims, cuts, low, high):
    gain = 1.0
    for position, parts in cuts:
        draws = jax.random.uniform(jax.random.fold_in(jax.random.fold_in(own_key, 6), position), (parts,), jnp.float32, low / len(cuts), high / len(cuts))
        gain = gain * jnp.repeat(jnp.exp(draws), dims[position] // parts).reshape((-1,) + (1,) * (len(dims) - 1 - position))
    return gain


def normal_values(stream_key, shape, deviation, most, cuts=(), kind=jnp.bfloat16):
    factor_of = block_levels(stream_key, shape, cuts, -0.22, 0.18) if cuts else 1.0
    drawn = jax.random.normal(stream_key, shape, jnp.float32) * deviation * factor_of
    return jnp.minimum(jnp.maximum(drawn, -most), most).astype(kind)


def setup_inputs(seed: int = 0, part: int = 0) -> dict:
    key_list = jax.random.split(jax.random.key(seed), 4)
    part_splits = jax.random.split(jax.random.fold_in(key_list[3], part), 4)
    return {
        "voltages": normal_values(part_splits[0], (INPUTS, FRAMES * NFFT), 1.0, 6.0, ((0, 8), (1, 2))),
        "channels": draw_channels(jax.random.fold_in(key_list[3], 71), part),
        "tile_pairs": draw_tile_pairs(jax.random.fold_in(key_list[3], 71), part),
    }


def dft_table(channels, length):
    samples = jnp.arange(length, dtype=jnp.int32)
    phase = channels[:, None] * samples[None, :] % length
    angle = 2.0 * jnp.pi / length * phase.astype(jnp.float32)
    window = 0.5 - 0.5 * jnp.cos(2.0 * jnp.pi / length * samples.astype(jnp.float32))
    scale = 1.0 / jnp.sqrt(jnp.float32(0.375 * length))
    table = jnp.concatenate([window * jnp.cos(angle), -window * jnp.sin(angle)], 0) * scale
    return table.astype(jnp.bfloat16)

def reference(voltages, channels, tile_pairs):
    table = dft_table(channels, NFFT)
    blocks = voltages.reshape(INPUTS // TILE, TILE * FRAMES, NFFT)

    def transform(block):
        return jnp.dot(table, block.T, preferred_element_type=jnp.float32).astype(jnp.bfloat16)
    spectra = lax.map(transform, blocks)
    spectra = spectra.reshape(INPUTS // TILE, 2, SEL, TILE, FRAMES)
    spectra = spectra.transpose(2, 1, 0, 3, 4).reshape(SEL, 2, INPUTS, FRAMES)

    def one_channel(spec):

        def one_pair(pair):
            first = lax.dynamic_slice_in_dim(spec, (pair[0] * TILE).astype(jnp.int32), TILE, 1).reshape(2 * TILE, FRAMES)
            second = lax.dynamic_slice_in_dim(spec, (pair[1] * TILE).astype(jnp.int32), TILE, 1).reshape(2 * TILE, FRAMES)
            prod = jnp.dot(first, second.T, preferred_element_type=jnp.float32)
            real = prod[:TILE, :TILE] + prod[TILE:, TILE:]
            imag = prod[:TILE, TILE:] - prod[TILE:, :TILE]
            return (jnp.concatenate([real, imag], 1) / FRAMES).astype(jnp.bfloat16)
        return lax.map(one_pair, tile_pairs)
    return lax.map(one_channel, spectra)
```

```python
import functools

import jax
import jax.numpy as jnp
from jax import lax
from jax.experimental import pallas as pl
from jax.experimental.pallas import tpu as pltpu
from jax.sharding import PartitionSpec as P

TILE = 64
NFFT = 2048
LANES = 128
MESH = pl.DeviceIdType.MESH


def cos_sin(multiplier, steps):
    phase = lax.rem(multiplier * steps, NFFT)
    angle = (2.0 * jnp.pi / NFFT) * phase.astype(jnp.float32)
    return jnp.cos(angle), jnp.sin(angle)


def fill_table(channels_ref, table):
    count = channels_ref.shape[0]
    highs = NFFT // LANES
    scale = 1.0 / jnp.sqrt(jnp.float32(0.375 * NFFT))
    channels = channels_ref[...]
    low = lax.broadcasted_iota(jnp.int32, (count, LANES), 1)
    low_cos, low_sin = cos_sin(channels, low)
    high_cos, high_sin = cos_sin(channels, LANES * low)
    win_low = lax.broadcasted_iota(jnp.int32, (8, LANES), 1)
    win_cos, win_sin = cos_sin(1, win_low)
    win_high_cos, win_high_sin = cos_sin(1, LANES * win_low)
    for high in range(highs):
        columns = slice(high * LANES, (high + 1) * LANES)
        wc, ws = win_high_cos[:, high : high + 1], win_high_sin[:, high : high + 1]
        window = (0.5 - 0.5 * (win_cos * wc - win_sin * ws)) * scale
        window = jnp.broadcast_to(window[:1], (count, LANES))
        hc, hs = high_cos[:, high : high + 1], high_sin[:, high : high + 1]
        real = window * (low_cos * hc - low_sin * hs)
        imag = -window * (low_sin * hc + low_cos * hs)
        table[:, columns] = jnp.concatenate([real, imag], 0).astype(jnp.bfloat16)


def transform_kernel(
    n_wide, n_tm, channels_ref, v_hbm, out, blocks, table, staged, send, in_sems, send_sems, recv_sems, own_sem
):
    frames, in_dev, _ = blocks.shape
    count = channels_ref.shape[0]
    rows = 2 * frames
    wide, tm = lax.axis_index("wide"), lax.axis_index("tm")
    me = wide * n_tm + tm
    peers = n_wide * n_tm

    loads = [
        pltpu.make_async_copy(
            v_hbm.at[:, pl.ds(f * NFFT, NFFT)], blocks.at[f], in_sems.at[f]
        )
        for f in range(frames)
    ]
    for load in loads:
        load.start()

    barrier = pltpu.get_barrier_semaphore()

    def greet(k, carry):
        peer = lax.rem(me + k, peers)
        pl.semaphore_signal(
            barrier,
            inc=1,
            device_id={"wide": peer // n_tm, "tm": lax.rem(peer, n_tm)},
            device_id_type=MESH,
        )
        return carry

    lax.fori_loop(1, peers, greet, 0)

    fill_table(channels_ref, table)

    for f in range(frames):
        loads[f].wait()
        spectrum = lax.dot_general(
            table[...], blocks[f], (((1,), (1,)), ((), ())), preferred_element_type=jnp.float32
        )
        for q in range(2):
            staged[:, q * frames + f, :] = spectrum[q * count : (q + 1) * count]
    send[...] = staged[...].astype(jnp.bfloat16)

    pl.semaphore_wait(barrier, peers - 1)
    per_dev = count // peers

    def copy_to(k):
        peer = lax.rem(me + k, peers)
        return pltpu.make_async_remote_copy(
            src_ref=send.at[pl.ds(peer * per_dev, per_dev)],
            dst_ref=out.at[wide, tm],
            send_sem=send_sems.at[k],
            recv_sem=recv_sems.at[k],
            device_id={"wide": peer // n_tm, "tm": lax.rem(peer, n_tm)},
            device_id_type=MESH,
        )

    def start(k, carry):
        copy_to(k).start()
        return carry

    def wait(k, carry):
        copy_to(k).wait()
        return carry

    lax.fori_loop(1, peers, start, 0)
    own = pltpu.make_async_copy(send.at[pl.ds(me * per_dev, per_dev)], out.at[wide, tm], own_sem)
    own.start()
    own.wait()
    lax.fori_loop(1, peers, wait, 0)


def transform(voltages, channels, n_wide, n_tm):
    in_dev, samples = voltages.shape
    frames = samples // NFFT
    count = channels.shape[0]
    peers = n_wide * n_tm
    rows = 2 * frames
    return pl.pallas_call(
        functools.partial(transform_kernel, n_wide, n_tm),
        out_shape=jax.ShapeDtypeStruct((n_wide, n_tm, count // peers, rows, in_dev), jnp.bfloat16),
        in_specs=[
            pl.BlockSpec(memory_space=pltpu.VMEM),
            pl.BlockSpec(memory_space=pltpu.HBM),
        ],
        out_specs=pl.BlockSpec(memory_space=pltpu.VMEM),
        scratch_shapes=[
            pltpu.VMEM((frames, in_dev, NFFT), jnp.bfloat16),
            pltpu.VMEM((2 * count, NFFT), jnp.bfloat16),
            pltpu.VMEM((count, rows, in_dev), jnp.float32),
            pltpu.VMEM((count, rows, in_dev), jnp.bfloat16),
            pltpu.SemaphoreType.DMA((frames,)),
            pltpu.SemaphoreType.DMA((peers,)),
            pltpu.SemaphoreType.DMA((peers,)),
            pltpu.SemaphoreType.DMA,
        ],
        compiler_params=pltpu.CompilerParams(collective_id=0, has_side_effects=True),
        name="transform",
    )(channels.reshape(count, 1), voltages)


def correlate_kernel(frames, chunk, pairs_ref, spectra, out, left, right, products, sems):
    groups, n_tm, rows, in_group = spectra.shape
    half = rows // 2
    npairs = out.shape[0]
    for g in range(groups):
        blocks = [spectra[g, t].astype(jnp.float32) for t in range(n_tm)]
        plain = jnp.concatenate(blocks, 0)
        swapped = jnp.concatenate([x for b in blocks for x in (b[half:], -b[:half])], 0)
        left[g * in_group : (g + 1) * in_group, :] = plain.T.astype(jnp.bfloat16)
        for j in range(in_group // TILE):
            columns = slice(j * TILE, (j + 1) * TILE)
            both = jnp.concatenate([plain[:, columns], swapped[:, columns]], 1)
            right[g * (in_group // TILE) + j] = both.astype(jnp.bfloat16)

    copies = []
    for c in range(npairs // chunk):
        for p in range(c * chunk, (c + 1) * chunk):
            first = left[pl.ds(pl.multiple_of(pairs_ref[0, p] * TILE, TILE), TILE), :]
            second = right[pairs_ref[1, p]]
            sums = jnp.dot(first, second, preferred_element_type=jnp.float32)
            products[p] = (sums * (1.0 / frames)).astype(jnp.bfloat16)
        span = pl.ds(c * chunk, chunk)
        copy = pltpu.make_async_copy(products.at[span], out.at[span], sems.at[c])
        copy.start()
        copies.append(copy)
    for copy in copies:
        copy.wait()


def correlate(spectra, pairs, frames):
    groups, n_tm, rows, in_group = spectra.shape
    npairs = pairs.shape[1]
    inputs = groups * in_group
    depth = n_tm * rows
    chunk = 16 if npairs % 16 == 0 else npairs
    return pl.pallas_call(
        functools.partial(correlate_kernel, frames, chunk),
        out_shape=jax.ShapeDtypeStruct((npairs, TILE, 2 * TILE), jnp.bfloat16),
        in_specs=[
            pl.BlockSpec(memory_space=pltpu.SMEM),
            pl.BlockSpec(memory_space=pltpu.VMEM),
        ],
        out_specs=pl.BlockSpec(memory_space=pltpu.HBM),
        scratch_shapes=[
            pltpu.VMEM((inputs, depth), jnp.bfloat16),
            pltpu.VMEM((inputs // TILE, depth, 2 * TILE), jnp.bfloat16),
            pltpu.VMEM((npairs, TILE, 2 * TILE), jnp.bfloat16),
            pltpu.SemaphoreType.DMA((npairs // chunk,)),
        ],
        name="correlate",
    )(pairs, spectra)


def shards(voltages, channels, tile_pairs):
    n_wide = lax.axis_size("wide")
    n_tm = lax.axis_size("tm")
    in_dev = voltages.shape[0]
    frames_all = voltages.shape[1] // NFFT * n_tm
    per_dev = channels.shape[0] // (n_wide * n_tm)
    turned = transform(voltages, channels, n_wide, n_tm)
    visibility = []
    for s in range(per_dev):
        spectra = turned[:, :, s]
        if in_dev % TILE:
            rows = spectra.shape[2]
            spectra = spectra.transpose(1, 2, 0, 3).reshape(1, n_tm, rows, n_wide * in_dev)
        visibility.append(correlate(spectra, tile_pairs.T, frames_all))
    return jnp.stack(visibility)


def solution(mesh):
    return jax.shard_map(
        shards,
        mesh=mesh,
        in_specs=(P("wide", ("grp", "tm")), P(), P()),
        out_specs=P(("grp", "wide", "tm"), None, None, None),
        check_vma=False,
    )
```

```python
import functools

import jax
import jax.numpy as jnp
from jax import lax
from jax.experimental import pallas as pl
from jax.experimental.pallas import tpu as pltpu
from jax.sharding import PartitionSpec as P

TILE = 64
NFFT = 2048
LANES = 128
SUBLANES = 8
OUT = pltpu.HBM
UNROLL = 16
KSPLIT = 1
GROUP = 2
MAXCHUNKS = 1
MESH = pl.DeviceIdType.MESH


def cos_sin(multiplier, steps):
    phase = lax.rem(multiplier * steps, NFFT)
    angle = (2.0 * jnp.pi / NFFT) * phase.astype(jnp.float32)
    return jnp.cos(angle), jnp.sin(angle)


def fill_table(channels_ref, table):
    count = channels_ref.shape[1]
    highs = NFFT // LANES
    scale = 1.0 / jnp.sqrt(jnp.float32(0.375 * NFFT))
    square = (count, count)
    diagonal = lax.broadcasted_iota(jnp.int32, square, 0) == lax.broadcasted_iota(jnp.int32, square, 1)
    row = jnp.broadcast_to(channels_ref[...].astype(jnp.float32), square)
    channels = jnp.sum(jnp.where(diagonal, row, 0.0), axis=1, keepdims=True).astype(jnp.int32)
    low = lax.broadcasted_iota(jnp.int32, (count, LANES), 1)
    low_cos, low_sin = cos_sin(channels, low)
    high_cos, high_sin = cos_sin(channels, LANES * low)
    win_low = lax.broadcasted_iota(jnp.int32, (8, LANES), 1)
    win_cos, win_sin = cos_sin(1, win_low)
    win_high_cos, win_high_sin = cos_sin(1, LANES * win_low)
    for high in range(highs):
        columns = slice(high * LANES, (high + 1) * LANES)
        wc, ws = win_high_cos[:, high : high + 1], win_high_sin[:, high : high + 1]
        window = (0.5 - 0.5 * (win_cos * wc - win_sin * ws)) * scale
        window = jnp.broadcast_to(window[:1], (count, LANES))
        hc, hs = high_cos[:, high : high + 1], high_sin[:, high : high + 1]
        real = window * (low_cos * hc - low_sin * hs)
        imag = -window * (low_sin * hc + low_cos * hs)
        table[:, columns] = jnp.concatenate([real, imag], 0).astype(jnp.bfloat16)


def transformed(table, block):
    half = NFFT // KSPLIT
    return sum(
        lax.dot_general(
            table[:, k : k + half],
            block[:, k : k + half],
            (((1,), (1,)), ((), ())),
            preferred_element_type=jnp.float32,
        )
        for k in range(0, NFFT, half)
    )


def transform_kernel(
    n_wide, n_tm, channels_hbm, v_hbm, out, channels, blocks, table, staged, send, in_sems, send_sem, recv_sem
):
    frames, in_dev, _ = blocks.shape
    chunks, count, rows, _ = send.shape
    part = frames // chunks
    group = GROUP if part % GROUP == 0 else 1
    wide, tm = lax.axis_index("wide"), lax.axis_index("tm")
    me = wide * n_tm + tm
    peers = n_wide * n_tm
    per_dev = count // peers

    fetch = pltpu.make_async_copy(channels_hbm, channels, in_sems.at[frames])
    fetch.start()
    loads = [
        pltpu.make_async_copy(
            v_hbm.at[:, pl.ds(f * NFFT, NFFT)], blocks.at[f], in_sems.at[f]
        )
        for f in range(frames)
    ]
    for load in loads:
        load.start()

    def device(peer):
        return {"wide": peer // n_tm, "tm": lax.rem(peer, n_tm)}

    barrier = pltpu.get_barrier_semaphore()

    def greet(k, carry):
        peer = lax.rem(me + k, peers)
        pl.semaphore_signal(barrier, inc=1, device_id=device(peer), device_id_type=MESH)
        return carry

    lax.fori_loop(1, peers, greet, 0)

    fetch.wait()
    fill_table(channels, table)

    upper = 2 * wide // n_wide
    own_turn = upper * me + (1 - upper) * (peers - 1 - me)

    def peer_at(k):
        turn = k + (k + peers - own_turn) // peers
        return upper * turn + (1 - upper) * (peers - 1 - turn)

    def copy_to(chunk, peer):
        return pltpu.make_async_remote_copy(
            src_ref=send.at[chunk, pl.ds(peer * per_dev, per_dev)],
            dst_ref=out.at[wide, tm, chunk],
            send_sem=send_sem,
            recv_sem=recv_sem,
            device_id=device(peer),
            device_id_type=MESH,
        )

    for c in range(chunks):
        for f0 in range(c * part, (c + 1) * part, group):
            members = range(f0, f0 + group)
            for f in members:
                loads[f].wait()
            spectrum = [transformed(table, blocks.at[f]) for f in members]
            for f, values in zip(members, spectrum):
                for q in range(2):
                    staged[c, :, q * part + f - c * part, :] = values[q * count : (q + 1) * count]
        send[c] = staged[c].astype(jnp.bfloat16)

        if c == 0:
            pl.semaphore_wait(barrier, peers - 1)

        def start(k, carry):
            copy_to(c, peer_at(k)).start()
            return carry

        lax.fori_loop(0, peers - 1, start, 0, unroll=peers <= UNROLL)
        own = pltpu.make_async_copy(
            send.at[c, pl.ds(me * per_dev, per_dev)], out.at[wide, tm, c], recv_sem
        )
        own.start()

    others = send.at[:, pl.ds(0, (peers - 1) * per_dev)]
    pltpu.make_async_copy(others, others, send_sem).wait()
    pltpu.make_async_copy(send, send, recv_sem).wait()


def transform(voltages, channels, n_wide, n_tm):
    in_dev, samples = voltages.shape
    frames = samples // NFFT
    count = channels.shape[0]
    peers = n_wide * n_tm
    chunks = min(MAXCHUNKS, max(1, 2 * frames // SUBLANES))
    rows = 2 * frames // chunks
    return pl.pallas_call(
        functools.partial(transform_kernel, n_wide, n_tm),
        out_shape=jax.ShapeDtypeStruct((n_wide, n_tm, chunks, count // peers, rows, in_dev), jnp.bfloat16),
        in_specs=[pl.BlockSpec(memory_space=pltpu.HBM)] * 2,
        out_specs=pl.BlockSpec(memory_space=OUT),
        scratch_shapes=[
            pltpu.VMEM((1, count), jnp.int32),
            pltpu.VMEM((frames, in_dev, NFFT), jnp.bfloat16),
            pltpu.VMEM((2 * count, NFFT), jnp.bfloat16),
            pltpu.VMEM((chunks, count, rows, in_dev), jnp.float32),
            pltpu.VMEM((chunks, count, rows, in_dev), jnp.bfloat16),
            pltpu.SemaphoreType.DMA((frames + 1,)),
            pltpu.SemaphoreType.DMA,
            pltpu.SemaphoreType.DMA,
        ],
        compiler_params=pltpu.CompilerParams(collective_id=0, has_side_effects=True),
        name="transform",
    )(channels.reshape(1, count), voltages)


def correlate_kernel(frames, chunk, pairs_ref, spectra, out, left, right, products, sems):
    groups, n_tm, chunks, rows, in_group = spectra.shape
    half = rows // 2
    npairs = out.shape[0]
    for g in range(groups):
        blocks = [spectra[g, t, c].astype(jnp.float32) for t in range(n_tm) for c in range(chunks)]
        plain = jnp.concatenate(blocks, 0)
        swapped = jnp.concatenate([x for b in blocks for x in (b[half:], -b[:half])], 0)
        left[g * in_group : (g + 1) * in_group, :] = plain.T.astype(jnp.bfloat16)
        for j in range(in_group // TILE):
            columns = slice(j * TILE, (j + 1) * TILE)
            both = jnp.concatenate([plain[:, columns], swapped[:, columns]], 1)
            right[g * (in_group // TILE) + j] = both.astype(jnp.bfloat16)

    copies = []
    for c in range(npairs // chunk):
        for p in range(c * chunk, (c + 1) * chunk):
            first = left[pl.ds(pl.multiple_of(pairs_ref[0, p] * TILE, TILE), TILE), :]
            second = right[pairs_ref[1, p]]
            sums = jnp.dot(first, second, preferred_element_type=jnp.float32)
            products[p] = (sums * (1.0 / frames)).astype(jnp.bfloat16)
        span = pl.ds(c * chunk, chunk)
        copy = pltpu.make_async_copy(products.at[span], out.at[span], sems.at[c])
        copy.start()
        copies.append(copy)
    for copy in copies:
        copy.wait()


def correlate(spectra, pairs, frames):
    groups, n_tm, chunks, rows, in_group = spectra.shape
    npairs = pairs.shape[1]
    inputs = groups * in_group
    depth = n_tm * chunks * rows
    chunk = 16 if npairs % 16 == 0 else npairs
    return pl.pallas_call(
        functools.partial(correlate_kernel, frames, chunk),
        out_shape=jax.ShapeDtypeStruct((npairs, TILE, 2 * TILE), jnp.bfloat16),
        in_specs=[
            pl.BlockSpec(memory_space=pltpu.SMEM),
            pl.BlockSpec(memory_space=pltpu.VMEM),
        ],
        out_specs=pl.BlockSpec(memory_space=pltpu.HBM),
        scratch_shapes=[
            pltpu.VMEM((inputs, depth), jnp.bfloat16),
            pltpu.VMEM((inputs // TILE, depth, 2 * TILE), jnp.bfloat16),
            pltpu.VMEM((npairs, TILE, 2 * TILE), jnp.bfloat16),
            pltpu.SemaphoreType.DMA((npairs // chunk,)),
        ],
        name="correlate",
    )(pairs, spectra)


def shards(voltages, channels, tile_pairs):
    n_wide = lax.axis_size("wide")
    n_tm = lax.axis_size("tm")
    in_dev = voltages.shape[0]
    frames_all = voltages.shape[1] // NFFT * n_tm
    per_dev = channels.shape[0] // (n_wide * n_tm)
    turned = transform(voltages, channels, n_wide, n_tm)
    visibility = []
    for s in range(per_dev):
        spectra = turned[:, :, :, s]
        if in_dev % TILE:
            chunks, rows = spectra.shape[2:4]
            spectra = spectra.transpose(1, 2, 3, 0, 4).reshape(1, n_tm, chunks, rows, n_wide * in_dev)
        visibility.append(correlate(spectra, tile_pairs.T, frames_all))
    return jnp.stack(visibility)


def solution(mesh):
    return jax.shard_map(
        shards,
        mesh=mesh,
        in_specs=(P("wide", ("grp", "tm")), P(), P()),
        out_specs=P(("grp", "wide", "tm"), None, None, None),
        check_vma=False,
    )
```
